128 devices in a mesh: row: 8 (over x, z_hi), col: 16 (over z_lo, y, core).
Axes of the slice: x: 4, y: 4, z: 4 (z_hi: 2, z_lo: 2; z = z_hi * 2 + z_lo), core: 2. Of those that a mesh axis runs over, the one named last changes fastest.
Arguments:
- pair_state: bfloat16 [768, 768, 128], P(('row', 'col')), may hold values from -6 to 6
- single_rep: bfloat16 [16, 768, 768], P(None, ('row', 'col')), may hold values from -64 to 64
- token_mask: int32 [768], replicated, may hold values 0 or 1
- chain_ids: int32 [768], replicated, may hold values from 0 to 3, never falling along the last dimension, each value on 1 to 384 neighbouring positions
- pair_gain: float32 [128], replicated, may hold values from 0.1 to 1.9
- mix_gain: float32 [128], replicated, may hold values from 0.1 to 1.9
- left_weight: bfloat16 [128, 256], replicated, may hold values from -0.5 to 0.5
- right_weight: bfloat16 [128, 256], replicated, may hold values from -0.5 to 0.5
- gate_weight: bfloat16 [128, 128], replicated, may hold values from -0.5 to 0.5
- out_weight: bfloat16 [128, 128], replicated, may hold values from -0.5 to 0.5
- bias_weight: bfloat16 [128, 16], replicated, may hold values from -1.5 to 1.5
- token_weight: bfloat16 [768, 2304], replicated, may hold values from -0.21875 to 0.21875
- merge_weight: bfloat16 [768, 768], replicated, may hold values from -0.625 to 0.625
Outputs:
- pair_tiles: bfloat16 [768, 8, 16, 6, 128], P('row', None, 'col')
- attention_out: bfloat16 [16, 768, 768], P(None, ('row', 'col'))
The draws below stay inside these ranges and needn't reach their ends.
Inputs may be any that keep to these rules, and one draw needn't show every extreme that they name: chain_ids never falls along the tokens; a chain holds 1 to 384 tokens.
All inputs are finite; a program needn't handle non-finite values.
Results may differ from the reference program's by a relative error of at most 0.034.
Values may be sent and summed in bfloat16 or wider, within the bound.
A program may use at most 256 MiB of HBM per device.

```python
import math
import jax
import jax.numpy as jnp
import numpy as np
from jax import lax

C = 128
HEADS = 16
HEAD_DIM = 48
D = 768
SAMPLES = 16
TOK_FLAT = 6
TOKENS = 768
N_ROW = 8
N_COL = 16


def draw_single_rep(key, part):
    full_shape = (SAMPLES, TOKENS, D)
    base_key = jax.random.fold_in(jax.random.fold_in(key, 11), 0)
    return jnp.clip(jax.random.normal(base_key, full_shape, jnp.float32), -6.0, 6.0).astype(jnp.bfloat16)


def with_ends(values, rng, smallest, top_value):
    extent = values.shape
    index_at = [jax.random.randint(jax.random.fold_in(rng, axis), (), 0, extent[axis]) for axis in range(len(extent))]
    values = values.at[tuple(index_at)].set(smallest)
    longest = extent.index(max(extent))
    index_at[longest] = (index_at[longest] + 1) % extent[longest]
    return values.at[tuple(index_at)].set(top_value)


def steps_of(rng, dims, shards, low, largest):
    level, own = 1.0, jax.random.fold_in(rng, 6)
    for axis_at, blocks in shards:
        steps = jnp.exp(jax.random.uniform(jax.random.fold_in(own, axis_at), (blocks,), jnp.float32, low / len(shards), largest / len(shards)))
        level = level * jnp.repeat(steps, dims[axis_at] // blocks).reshape([-1 if axis == axis_at else 1 for axis in range(len(dims))])
    return level


def split_up(number_of, total, limit, skew):
    weights = [(1 << 20) // math.isqrt(standing ** skew) + 1 for standing in range(2, number_of + 1)]
    rest, counts = total - limit - (number_of - 1), [1] * (number_of - 1)
    while rest > 0:
        candidates = [i for i in range(number_of - 1) if counts[i] < limit]
        whole, remaining = sum([weights[i] for i in candidates]), rest
        for i in candidates:
            extra = min(limit - counts[i], max(1, remaining * weights[i] // whole), rest)
            counts[i] = counts[i] + extra
            rest = rest - extra
    return np.array([limit] + counts)


def uneven_parts(rng, number_of, total, most, slope):
    if number_of == 2:
        one = jax.random.randint(rng, (), max(1, total - most), min(most, total - 1) + 1)
        return jnp.stack([one, total - one])
    tallies = jnp.asarray(split_up(number_of, total, most, slope), jnp.int32)
    pairs = (number_of - 1) // 2
    giver, sink = tallies[1:1 + 2 * pairs:2], tallies[2:2 + 2 * pairs:2]
    slack = jnp.minimum(giver - 1, most - sink)
    moved = jax.random.randint(jax.random.fold_in(rng, 1), (pairs,), 0, 1 << 20) % (slack + 1)
    tallies = tallies.at[1:1 + 2 * pairs:2].set(giver - moved).at[2:2 + 2 * pairs:2].set(sink + moved)
    return tallies[jax.random.permutation(jax.random.fold_in(rng, 2), number_of)]


def gaussian(rng, shape, deviation, limit, cuts=(), kind=jnp.bfloat16):
    values = jax.random.normal(rng, shape, jnp.float32) * deviation
    if len(cuts) > 0:
        values = steps_of(rng, shape, cuts, -0.22, 0.18) * values
    return jnp.clip(values, min=-limit, max=limit).astype(kind)


def setup_inputs(seed: int = 0) -> dict:
    key_of = jax.random.split(jax.random.key(seed), 14)
    pair_state = gaussian(key_of[0], (TOKENS, TOKENS, C), 1.0, 6.0, ((0, 128),))
    single_rep = draw_single_rep(jax.random.fold_in(key_of[13], 71), 0)
    token_mask = with_ends((jax.random.randint(key_of[2], (TOKENS,), 0, 8) < 7).astype(jnp.int32), jax.random.fold_in(key_of[2], 1), 0, 1)
    chain_ids = jnp.searchsorted(jnp.cumsum(uneven_parts(key_of[3], 4, TOKENS, TOKENS // 2, 0)), jnp.arange(TOKENS), side="right").astype(jnp.int32)
    pair_gain = jnp.clip(1.0 + 0.18 * jax.random.normal(key_of[4], (C,), jnp.float32), 0.1, 1.9)
    mix_gain = jnp.clip(1.0 + 0.18 * jax.random.normal(key_of[5], (C,), jnp.float32), 0.1, 1.9)
    left_weight = gaussian(key_of[6], (C, 2 * C), C ** -0.5, 0.5)
    right_weight = gaussian(key_of[7], (C, 2 * C), C ** -0.5, 0.5)
    gate_weight = gaussian(key_of[8], (C, C), C ** -0.5, 0.5)
    out_weight = gaussian(key_of[9], (C, C), C ** -0.5, 0.5)
    bias_weight = gaussian(key_of[10], (C, HEADS), 0.25, 1.5)
    token_weight = gaussian(key_of[11], (D, 3 * D), D ** -0.5, 0.21875)
    merge_weight = gaussian(key_of[12], (D, D), (D // 8) ** -0.5, 0.625)
    return {"pair_state": pair_state, "single_rep": single_rep, "token_mask": token_mask, "chain_ids": chain_ids, "pair_gain": pair_gain, "mix_gain": mix_gain, "left_weight": left_weight, "right_weight": right_weight, "gate_weight": gate_weight, "out_weight": out_weight, "bias_weight": bias_weight, "token_weight": token_weight, "merge_weight": merge_weight}


epsilon = 1e-05

def normalize(values, norm_gain):
    floats = values.astype(jnp.float32)
    centered = floats - lax.optimization_barrier(jnp.mean(floats, axis=-1, keepdims=True))
    variance = lax.optimization_barrier(jnp.mean(centered * centered, axis=-1, keepdims=True))
    scaled = centered * lax.rsqrt(variance + epsilon)
    if norm_gain is None:
        return scaled
    return scaled * norm_gain

def gated_branch(normed, weight, pair_mask):
    half_width = weight.shape[0]
    hidden = jnp.dot(normed.reshape(-1, half_width), weight, preferred_element_type=jnp.float32)
    hidden = hidden.reshape(normed.shape[0], normed.shape[1], 2 * half_width)
    return (jax.nn.sigmoid(hidden[..., :half_width]) * hidden[..., half_width:] * pair_mask[..., None]).astype(jnp.bfloat16)

def project_pairs(normed, weight):
    result = jnp.dot(normed.reshape(-1, normed.shape[-1]), weight, preferred_element_type=jnp.float32)
    return result.reshape(normed.shape[0], normed.shape[1], weight.shape[1])

def reference(pair_state, single_rep, token_mask, chain_ids, pair_gain, mix_gain, left_weight, right_weight, gate_weight, out_weight, bias_weight, token_weight, merge_weight):
    valid_all = (token_mask == 1).astype(jnp.float32)
    pair_mask = valid_all[:, None] * valid_all[None, :]
    normed = normalize(pair_state, pair_gain).astype(jnp.bfloat16)
    left_edges = gated_branch(normed, left_weight, pair_mask)
    right_edges = gated_branch(normed, right_weight, pair_mask)
    mixed_pairs = jnp.einsum('ikc,jkc->ijc', left_edges.astype(jnp.float32), right_edges.astype(jnp.float32))
    mixed_norm = normalize(mixed_pairs, mix_gain).astype(jnp.bfloat16)
    gate_value = jax.nn.sigmoid(project_pairs(normed, gate_weight))
    update = project_pairs(mixed_norm, out_weight)
    pair_new = (pair_state.astype(jnp.float32) + gate_value * update).astype(jnp.bfloat16)
    bias_input = normalize(pair_new, None).astype(jnp.bfloat16)
    pair_bias = jnp.transpose(project_pairs(bias_input, bias_weight), (2, 0, 1))
    projected = jnp.dot(single_rep.reshape(-1, D), token_weight, preferred_element_type=jnp.float32)
    projected = projected.astype(jnp.bfloat16).reshape(SAMPLES, TOKENS, 3 * D)
    token_ids = jnp.arange(TOKENS, dtype=jnp.int32)
    allowed = (valid_all[None, :] > 0.5) & (chain_ids[:, None] == chain_ids[None, :]) | (token_ids[:, None] == token_ids[None, :])
    score_scale = 1.0 / math.sqrt(HEAD_DIM)

    def attend(sample_block):
        query_heads = sample_block[:, :D].astype(jnp.float32).reshape(TOKENS, HEADS, HEAD_DIM)
        key_heads = sample_block[:, D:2 * D].astype(jnp.float32).reshape(TOKENS, HEADS, HEAD_DIM)
        value_heads = sample_block[:, 2 * D:].astype(jnp.float32).reshape(TOKENS, HEADS, HEAD_DIM)
        scores = jnp.einsum('ihd,jhd->hij', query_heads, key_heads) * score_scale + pair_bias
        row_max = lax.optimization_barrier(jnp.max(jnp.where(allowed[None], scores, -1e+30), axis=-1))
        weights = jnp.where(allowed[None], jnp.exp(scores - row_max[..., None]), 0.0).astype(jnp.bfloat16)
        totals = lax.optimization_barrier(jnp.sum(weights.astype(jnp.float32), axis=-1))
        summed = jnp.einsum('hij,jhd->ihd', weights.astype(jnp.float32), value_heads)
        attended = (summed / jnp.transpose(totals)[:, :, None]).astype(jnp.bfloat16).reshape(TOKENS, D)
        return jnp.dot(attended, merge_weight, preferred_element_type=jnp.float32).astype(jnp.bfloat16)
    attention_out = lax.map(attend, projected)
    return (pair_new.reshape(TOKENS, N_ROW, N_COL, TOK_FLAT, C), attention_out)
```

```python
import functools
import math

import jax
import jax.numpy as jnp
from jax import lax
from jax.experimental import pallas as pl
from jax.experimental.pallas import tpu as pltpu
from jax.sharding import PartitionSpec as P

epsilon = 1e-05
bf16 = jnp.bfloat16
f32 = jnp.float32
NT = (((1,), (1,)), ((), ()))
TN = (((0,), (0,)), ((), ()))


def norm_lanes(x):
    centered = x - jnp.mean(x, axis=-1, keepdims=True)
    variance = jnp.mean(centered * centered, axis=-1, keepdims=True)
    return centered * lax.rsqrt(variance + epsilon)


def swap01(x):
    return jnp.swapaxes(x, 0, 1)


class Exchange:
    def __init__(self, axis, size, source, target, landing, send_sem, recv_sem, local_sem):
        self.axis = axis
        self.size = size
        self.source = source
        self.target = target
        self.landing = landing
        self.send_sem = send_sem
        self.recv_sem = recv_sem
        self.local_sem = local_sem

    def me(self):
        return lax.axis_index(self.axis)

    def peer(self, step):
        return lax.rem(self.me() + step, self.size)

    def own(self):
        return pltpu.make_async_copy(
            self.source(self.me()), self.target(self.me()), self.local_sem
        )

    def copy(self, peer, sender):
        return pltpu.make_async_remote_copy(
            src_ref=self.source(peer),
            dst_ref=self.target(sender),
            send_sem=self.send_sem.at[peer],
            recv_sem=self.recv_sem.at[sender],
            device_id={self.axis: peer},
            device_id_type=pl.DeviceIdType.MESH,
        )

    def start(self):
        def step(p, carry):
            self.copy(self.peer(p), self.me()).start()
            return carry

        lax.fori_loop(1, self.size, step, 0)
        self.own().start()

    def wait_recv(self):
        self.own().wait()

        def step(p, carry):
            other = self.peer(p)
            self.copy(other, other).wait_recv()
            return carry

        lax.fori_loop(1, self.size, step, 0)

    def wait_send(self):
        def step(p, carry):
            other = self.peer(p)
            self.copy(other, other).wait_send()
            return carry

        lax.fori_loop(1, self.size, step, 0)


def kernel(
    rows,
    cols,
    pair_ref,
    single_ref,
    valid_ref,
    forbid_ref,
    pair_gain_ref,
    mix_gain_ref,
    left_ref,
    right_ref,
    gate_ref,
    out_w_ref,
    bias_ref,
    token_ref,
    merge_ref,
    tiles_out,
    attn_out,
    wt,
    send_a,
    recv_a,
    send_b,
    recv_l,
    recv_r,
    send_c,
    recv_c,
    send_d,
    recv_d,
    row_f,
    send_p,
    recv_p,
    pair_j,
    gate_j,
    proj,
    send_q,
    recv_q,
    query,
    send_k,
    recv_k,
    bias_j,
    send_e,
    recv_e,
    bias_t,
    bias_s,
    att,
    send_f,
    recv_f,
    *sems,
):
    flat = pair_ref.shape[0]
    tokens = pair_ref.shape[1]
    channels = pair_ref.shape[2]
    samples = single_ref.shape[0] // flat
    width = single_ref.shape[1]
    heads = cols
    head = width // heads
    block = flat * cols
    sem_iter = iter(sems)

    def exchange(axis, size, source, target):
        return Exchange(
            axis, size, source, target, None, next(sem_iter), next(sem_iter), next(sem_iter)
        )

    row = lax.axis_index("row")
    col = lax.axis_index("col")
    own = (row * cols + col) * flat

    ch8 = channels // cols
    ex_a = exchange(
        "col",
        cols,
        lambda p: send_a.at[:, :, pl.ds(pl.multiple_of(p * ch8, ch8), ch8), :],
        lambda s: recv_a.at[s],
    )
    ex_p = exchange("col", cols, lambda p: send_p.at[p], lambda s: recv_p.at[s])
    ex_q = exchange("col", cols, lambda p: send_q.at[p], lambda s: recv_q.at[s])
    ex_l = exchange(
        "row", rows, lambda p: send_b.at[p, 0], lambda s: recv_l.at[s, pl.ds(0, block)]
    )
    ex_r = exchange("row", rows, lambda p: send_b.at[p, 1], lambda s: recv_r.at[s])
    ex_k = exchange("row", rows, lambda p: send_k, lambda s: recv_k.at[s])
    ex_c = exchange("row", rows, lambda p: send_c.at[p], lambda s: recv_c.at[s])
    ex_d = exchange(
        "col",
        cols,
        lambda p: send_d.at[p],
        lambda s: recv_d.at[:, pl.ds(pl.multiple_of(s * ch8, ch8), ch8), :],
    )
    ex_e = exchange("col", cols, lambda p: send_e.at[p], lambda s: recv_e.at[s])
    ex_f = exchange("col", cols, lambda p: send_f.at[p], lambda s: recv_f.at[s])

    barrier = pltpu.get_barrier_semaphore()

    def greet(axis, size):
        def step(p, carry):
            peer = lax.rem(lax.axis_index(axis) + p, size)
            pl.semaphore_signal(
                barrier, inc=1, device_id={axis: peer}, device_id_type=pl.DeviceIdType.MESH
            )
            return carry

        lax.fori_loop(1, size, step, 0)

    greet("col", cols)
    greet("row", rows)

    two = 2 * channels
    wt[0:two, :] = left_ref[...].astype(f32).T.astype(bf16)
    wt[two : 2 * two, :] = right_ref[...].astype(f32).T.astype(bf16)
    token_lane = lax.broadcasted_iota(jnp.int32, (1, tokens), 1)
    gain = pair_gain_ref[...]
    chunk = 256

    def project(t, carry):
        valid = valid_ref[...]
        valid_own = jnp.sum(jnp.where(token_lane == own + t, valid, 0.0), axis=1, keepdims=True)
        for start in range(0, tokens, chunk):
            x = pair_ref[t, start : start + chunk, :].astype(f32)
            normed = (norm_lanes(x) * gain).astype(bf16)
            mask = valid[:, start : start + chunk] * valid_own
            for side in range(2):
                hidden = lax.dot_general(
                    wt[side * two : (side + 1) * two, :], normed, NT, preferred_element_type=f32
                )
                gated = jax.nn.sigmoid(hidden[:channels]) * hidden[channels:] * mask
                send_a[t, side, :, start : start + chunk] = gated.astype(bf16)
        return carry

    lax.fori_loop(0, flat, project, 0)
    pl.semaphore_wait(barrier, cols - 1 + rows - 1)
    ex_a.start()

    def pair_rows(t, carry):
        row_f[0:tokens, :] = pair_ref[t].astype(f32)

        def piece(n, inner):
            a = n // cols
            c = lax.rem(n, cols)
            send_p[c, t, a] = row_f[pl.ds(n * flat, 8), :].astype(bf16)
            return inner

        lax.fori_loop(0, rows * cols, piece, 0, unroll=8)
        return carry

    row_f[tokens : tokens + 8, :] = jnp.zeros((8, channels), f32)
    lax.fori_loop(0, flat, pair_rows, 0)
    ex_p.start()

    own_rows = flat * samples
    proj[...] = (
        jnp.dot(single_ref[...], token_ref[...], preferred_element_type=f32)
        .astype(bf16)
        .astype(f32)
    )
    lane = lax.broadcasted_iota(jnp.int32, (own_rows, 128), 1)

    def window(start, at):
        base = start // 128 * 128
        offset = start - base
        size = 128 if offset + head <= 128 else 256
        x = proj[:, base : base + size]
        shift = (at - offset) % size
        if shift:
            x = pltpu.roll(x, shift, 1)
        return x[:, :128]

    first = lane < head
    second = (lane >= head) & (lane < 2 * head)
    ones = jnp.where(lane == 2 * head, 1.0, 0.0)
    for h in range(heads):
        q = window(h * head, head)
        k = window(width + h * head, head)
        v = window(2 * width + h * head, 0)
        send_q[h, :, 0:128] = jnp.where(second, q, 0.0).astype(bf16)
        send_q[h, :, 128:256] = jnp.where(first, v, jnp.where(second, k, ones)).astype(bf16)
    ex_q.start()

    recv_l[:, block:128, :] = jnp.zeros((rows, 128 - block, tokens), bf16)
    ex_a.wait_recv()

    def to_channels(t, carry):
        at = pl.ds(pl.multiple_of(t * cols, cols), cols)
        for side in range(2):
            send_b[:, side, at, :] = swap01(recv_a[:, t, side])
        return carry

    lax.fori_loop(0, flat, to_channels, 0)
    ex_l.start()
    ex_r.start()

    ex_q.wait_recv()

    def to_samples(t, carry):
        at = pl.ds(pl.multiple_of(t * samples, samples), samples)
        put = pl.ds(pl.multiple_of(t * cols, cols), cols)
        x = swap01(recv_q[:, at, :])
        query[:, put, :] = x[:, :, 0:128]
        send_k[:, put, :] = x[:, :, 128:256]
        return carry

    lax.fori_loop(0, flat, to_samples, 0)
    ex_k.start()

    ex_p.wait_recv()

    def pair_columns(n, carry):
        a = n // flat
        t = lax.rem(n, flat)
        put = pl.ds(pl.multiple_of(t * cols, cols), cols)
        pair_j[a, :, put, :] = swap01(recv_p[:, t, a])
        return carry

    lax.fori_loop(0, rows * flat, pair_columns, 0)

    def gates(n, carry):
        a = n // flat
        t = lax.rem(n, flat)
        normed = (norm_lanes(pair_j[a, t].astype(f32)) * gain).astype(bf16)
        gate_j[n] = jax.nn.sigmoid(jnp.dot(normed, gate_ref[...], preferred_element_type=f32))
        return carry

    lax.fori_loop(0, rows * flat, gates, 0)

    ex_l.wait_recv()
    ex_r.wait_recv()
    part = tokens // 3

    def triangle(n, carry):
        lhs = recv_l[pl.ds(n * 2, 2)].reshape(256, tokens)
        for piece in range(3):
            rhs = recv_r[...].reshape(tokens, tokens)[piece * part : (piece + 1) * part]
            mixed = lax.dot_general(rhs, lhs, NT, preferred_element_type=f32).astype(bf16)
            send_c[n * 2, piece * part : (piece + 1) * part, :] = mixed[:, 0:128]
            send_c[n * 2 + 1, piece * part : (piece + 1) * part, :] = mixed[:, 128:256]
        return carry

    lax.fori_loop(0, rows // 2, triangle, 0)
    ex_c.start()
    ex_c.wait_recv()

    def to_pairs(n, carry):
        at = pl.ds(pl.multiple_of(n * cols, cols), cols)
        send_d[:, n] = swap01(recv_c[:, at, :])
        return carry

    lax.fori_loop(0, rows * flat, to_pairs, 0)
    ex_d.start()
    ex_d.wait_recv()

    mix_gain = mix_gain_ref[...]
    bias_w = bias_ref[...].astype(f32).T.astype(bf16)

    def update_columns(a, carry):
        new = []
        for t in range(flat):
            n = a * flat + t
            mixed = recv_d[n].astype(f32)
            centered = mixed - jnp.mean(mixed, axis=0, keepdims=True)
            variance = jnp.mean(centered * centered, axis=0, keepdims=True)
            mixed_norm = (centered * lax.rsqrt(variance + epsilon) * mix_gain).astype(bf16)
            update = lax.dot_general(mixed_norm, out_w_ref[...], TN, preferred_element_type=f32)
            pair_new = pair_j[a, t].astype(f32) + gate_j[n] * update[:block]
            pair_new = pair_new.astype(bf16).astype(f32)
            new.append(pair_new)
            bias_input = norm_lanes(pair_new).astype(bf16)
            bias_j[a, t, :, 0:block] = lax.dot_general(
                bias_w, bias_input, NT, preferred_element_type=f32
            )
        zero = jnp.zeros((block, channels), f32)
        stacked = swap01(jnp.stack(new + [zero] * (8 - flat), axis=0))
        for t in range(flat):
            tile = stacked[t * cols : (t + 1) * cols, 0:flat, :]
            tiles_out[:, t, a] = tile.astype(bf16)
        send_e[:, a] = swap01(bias_j[a])
        return carry

    bias_j[...] = jnp.zeros(bias_j.shape, f32)
    lax.fori_loop(0, rows, update_columns, 0)
    ex_e.start()
    ex_e.wait_recv()

    for a in range(rows):
        x = swap01(recv_e[:, a])
        bias_t[a * block : (a + 1) * block, :] = x[0:flat].reshape(block, 128)
    for n in range(tokens // 128):
        at = slice(n * 128, (n + 1) * 128)
        bias_s[:, at] = bias_t[at, :].T[0:block] + forbid_ref[:, at]
    ex_k.wait_recv()
    score_scale = 1.0 / math.sqrt(head)

    def attend(s, carry):
        keys = recv_k[:, s].reshape(tokens, 128)
        scores = lax.dot_general(query[s], keys, NT, preferred_element_type=f32)
        scores = scores * score_scale + bias_s[...]
        row_max = jnp.max(scores, axis=-1, keepdims=True)
        weights = jnp.exp(scores - row_max).astype(bf16)
        summed = jnp.dot(weights, keys, preferred_element_type=f32)
        att[s] = (summed / summed[:, 2 * head : 2 * head + 1]).astype(bf16)
        return carry

    lax.fori_loop(0, samples, attend, 0)

    def to_tokens(t, carry):
        at = pl.ds(pl.multiple_of(t * cols, cols), cols)
        put = pl.ds(pl.multiple_of(t * samples, samples), samples)
        send_f[:, put, :] = swap01(att[:, at, :])
        return carry

    lax.fori_loop(0, flat, to_tokens, 0)
    ex_f.start()
    ex_f.wait_recv()
    merged = jnp.zeros((own_rows, width), f32)
    for h in range(heads):
        merged = merged + jnp.dot(
            recv_f[h][:, :head],
            merge_ref[h * head : (h + 1) * head, :],
            preferred_element_type=f32,
        )
    attn_out[...] = swap01(merged.reshape(flat, samples, width)).astype(bf16)

    for ex in (ex_a, ex_p, ex_q, ex_l, ex_r, ex_k, ex_c, ex_d, ex_e, ex_f):
        ex.wait_send()


def shards(
    pair_state,
    single_rep,
    token_mask,
    chain_ids,
    pair_gain,
    mix_gain,
    left_weight,
    right_weight,
    gate_weight,
    out_weight,
    bias_weight,
    token_weight,
    merge_weight,
):
    rows = lax.axis_size("row")
    cols = lax.axis_size("col")
    row_index = lax.axis_index("row")
    flat, tokens, channels = pair_state.shape
    samples, _, width = single_rep.shape
    heads = bias_weight.shape[1]
    block = flat * cols

    def key_order(x):
        return x.reshape(rows, cols, flat).transpose(0, 2, 1)

    ids = key_order(jnp.arange(tokens, dtype=jnp.int32))
    chains = key_order(chain_ids)
    valid = token_mask == 1
    ids_rows = lax.dynamic_index_in_dim(ids, row_index, 0, False).reshape(block)
    chain_rows = lax.dynamic_index_in_dim(chains, row_index, 0, False).reshape(block)
    allowed = key_order(valid).reshape(1, tokens) & (
        chain_rows[:, None] == chains.reshape(1, tokens)
    ) | (ids_rows[:, None] == ids.reshape(1, tokens))
    forbid = jnp.where(allowed, 0.0, -1e30).astype(f32)
    single_rows = single_rep.transpose(1, 0, 2).reshape(flat * samples, width)

    def vmem(*shape, dtype=bf16):
        return pltpu.VMEM(shape, dtype)

    own_rows = flat * samples
    ch8 = channels // cols
    pieces = rows * flat
    scratch = [
        vmem(4 * channels, channels),
        vmem(flat, 2, channels, tokens),
        vmem(cols, flat, 2, ch8, tokens),
        vmem(ch8, 2, block, tokens),
        vmem(rows, 128, tokens),
        vmem(rows, block, tokens),
        vmem(rows, tokens, 128),
        vmem(rows, tokens, 128),
        vmem(cols, pieces, ch8, 128),
        vmem(pieces, channels, 128),
        vmem(tokens + 8, channels, dtype=f32),
        vmem(cols, flat, rows, 8, channels),
        vmem(cols, flat, rows, 8, channels),
        vmem(rows, 8, block, channels),
        vmem(pieces, block, channels, dtype=f32),
        vmem(own_rows, 3 * width, dtype=f32),
        vmem(cols, own_rows, 256),
        vmem(cols, own_rows, 256),
        vmem(samples, block, 128),
        vmem(samples, block, 128),
        vmem(rows, samples, block, 128),
        vmem(rows, 8, heads, 128, dtype=f32),
        vmem(cols, rows, 8, 128, dtype=f32),
        vmem(cols, rows, 8, 128, dtype=f32),
        vmem(tokens, 128, dtype=f32),
        vmem(block, tokens, dtype=f32),
        vmem(samples, block, 128),
        vmem(cols, own_rows, 128),
        vmem(cols, own_rows, 128),
    ]
    for size in (cols, cols, cols, rows, rows, rows, rows, cols, cols, cols):
        scratch += [
            pltpu.SemaphoreType.DMA((size,)),
            pltpu.SemaphoreType.DMA((size,)),
            pltpu.SemaphoreType.DMA,
        ]
    whole = pl.BlockSpec(memory_space=pltpu.VMEM)
    tiles, attention_out = pl.pallas_call(
        functools.partial(kernel, rows, cols),
        out_shape=(
            jax.ShapeDtypeStruct((cols, flat, rows, flat, channels), bf16),
            jax.ShapeDtypeStruct((samples, flat, width), bf16),
        ),
        in_specs=[whole] * 13,
        out_specs=(whole, whole),
        scratch_shapes=scratch,
        compiler_params=pltpu.CompilerParams(
            collective_id=0, has_side_effects=True, vmem_limit_bytes=60 * 1024 * 1024
        ),
    )(
        pair_state,
        single_rows,
        valid.astype(f32).reshape(1, tokens),
        forbid,
        pair_gain.reshape(1, channels),
        mix_gain.reshape(channels, 1),
        left_weight,
        right_weight,
        gate_weight,
        out_weight,
        bias_weight,
        token_weight,
        merge_weight,
    )
    return tiles.reshape(block, rows, 1, flat, channels), attention_out


def solution(mesh):
    in_specs = (
        P(("row", "col"), None, None),
        P(None, ("row", "col"), None),
        P(),
        P(),
        P(),
        P(),
        P(),
        P(),
        P(),
        P(),
        P(),
        P(),
        P(),
    )
    out_specs = (P("row", None, "col", None, None), P(None, ("row", "col"), None))
    return jax.shard_map(shards, mesh=mesh, in_specs=in_specs, out_specs=out_specs, check_vma=False)
```

```python
import functools
import math

import jax
import jax.numpy as jnp
from jax import lax
from jax.experimental import pallas as pl
from jax.experimental.pallas import tpu as pltpu
from jax.sharding import PartitionSpec as P

epsilon = 1e-05
bf16 = jnp.bfloat16
f32 = jnp.float32
NT = (((1,), (1,)), ((), ()))
TN = (((0,), (0,)), ((), ()))


def norm_lanes(x):
    centered = x - jnp.mean(x, axis=-1, keepdims=True)
    variance = jnp.mean(centered * centered, axis=-1, keepdims=True)
    return centered * lax.rsqrt(variance + epsilon)


def swap01(x):
    return jnp.swapaxes(x, 0, 1)


def pair_groups(rows):
    return max(1, rows // 2)


class Exchange:
    def __init__(self, axis, size, chunks, source, target, sems):
        self.axis = axis
        self.size = size
        self.chunks = chunks
        self.source = source
        self.target = target
        self.send_sem, self.recv_sem, self.local_sem = sems

    def me(self):
        return lax.axis_index(self.axis)

    def own(self, chunk):
        return pltpu.make_async_copy(
            self.source(self.me(), chunk), self.target(self.me(), chunk), self.local_sem.at[chunk]
        )

    def copy(self, peer, sender, chunk):
        return pltpu.make_async_remote_copy(
            src_ref=self.source(peer, chunk),
            dst_ref=self.target(sender, chunk),
            send_sem=self.send_sem.at[chunk, peer],
            recv_sem=self.recv_sem.at[chunk, sender],
            device_id={self.axis: peer},
            device_id_type=pl.DeviceIdType.MESH,
        )

    def each(self, act):
        def step(p, carry):
            act(lax.rem(self.me() + p, self.size))
            return carry

        lax.fori_loop(1, self.size, step, 0)

    def start(self, chunk=0):
        self.each(lambda other: self.copy(other, self.me(), chunk).start())
        self.own(chunk).start()

    def wait_recv(self, chunk=0):
        self.own(chunk).wait()
        self.each(lambda other: self.copy(other, other, chunk).wait_recv())

    def wait_send(self):
        def step(chunk, carry):
            self.each(lambda other: self.copy(other, other, chunk).wait_send())
            return carry

        lax.fori_loop(0, self.chunks, step, 0)


def kernel(
    rows,
    cols,
    pair_ref,
    single_ref,
    valid_ref,
    forbid_ref,
    pair_gain_ref,
    mix_gain_ref,
    left_ref,
    right_ref,
    gate_ref,
    out_w_ref,
    bias_ref,
    token_ref,
    merge_ref,
    tiles_out,
    attn_out,
    wt,
    send_a,
    recv_a,
    send_b,
    recv_l,
    recv_r,
    send_c,
    recv_c,
    send_d,
    recv_d,
    row_f,
    send_p,
    recv_p,
    pair_j,
    gate_j,
    proj,
    send_q,
    recv_q,
    query,
    send_k,
    recv_k,
    bias_j,
    send_e,
    recv_e,
    bias_t,
    bias_s,
    att,
    send_f,
    recv_f,
    *sems,
):
    flat = pair_ref.shape[0]
    tokens = pair_ref.shape[1]
    channels = pair_ref.shape[2]
    samples = single_ref.shape[0] // flat
    width = single_ref.shape[1]
    heads = cols
    head = width // heads
    block = flat * cols
    mixes = pair_groups(rows)
    group = rows // mixes
    sem_iter = iter(sems)

    def exchange(axis, size, chunks, source, target):
        three = next(sem_iter), next(sem_iter), next(sem_iter)
        return Exchange(axis, size, chunks, source, target, three)

    row = lax.axis_index("row")
    col = lax.axis_index("col")
    own = (row * cols + col) * flat
    ch8 = channels // cols

    def tile(p):
        return pl.ds(pl.multiple_of(p * ch8, ch8), ch8)

    def span(n, size):
        return pl.ds(pl.multiple_of(n * size, size), size)

    ex_a = exchange(
        "col", cols, flat, lambda p, t: send_a.at[t, :, tile(p), :], lambda s, t: recv_a.at[s, t]
    )
    ex_p = exchange("col", cols, 1, lambda p, _: send_p.at[p], lambda s, _: recv_p.at[s])
    ex_q = exchange("col", cols, 1, lambda p, _: send_q.at[p], lambda s, _: recv_q.at[s])
    ex_l = exchange(
        "row",
        rows,
        flat,
        lambda p, t: send_b.at[p, 0, span(t, cols)],
        lambda s, t: recv_l.at[s, span(t, cols)],
    )
    ex_r = exchange(
        "row",
        rows,
        flat,
        lambda p, t: send_b.at[p, 1, span(t, cols)],
        lambda s, t: recv_r.at[s, span(t, cols)],
    )
    ex_k = exchange("row", rows, 1, lambda p, _: send_k, lambda s, _: recv_k.at[s])
    ex_c = exchange(
        "row",
        rows,
        mixes,
        lambda p, n: send_c.at[p, span(n, group * block)],
        lambda s, n: recv_c.at[s, span(n, group * block)],
    )
    ex_d = exchange(
        "col",
        cols,
        mixes,
        lambda p, n: send_d.at[p, pl.ds(n * group * flat, group * flat)],
        lambda s, n: recv_d.at[pl.ds(n * group * flat, group * flat), tile(s), :],
    )
    ex_e = exchange(
        "col",
        cols,
        mixes,
        lambda p, n: send_e.at[p, pl.ds(n * group, group)],
        lambda s, n: recv_e.at[s, pl.ds(n * group, group)],
    )
    ex_f = exchange("col", cols, 1, lambda p, _: send_f.at[p], lambda s, _: recv_f.at[s])

    barrier = pltpu.get_barrier_semaphore()

    def greet(axis, size):
        def step(p, carry):
            peer = lax.rem(lax.axis_index(axis) + p, size)
            pl.semaphore_signal(
                barrier, inc=1, device_id={axis: peer}, device_id_type=pl.DeviceIdType.MESH
            )
            return carry

        lax.fori_loop(1, size, step, 0)

    two = 2 * channels
    gain = pair_gain_ref[...]
    own_rows = flat * samples

    def project():
        wt[0:two, :] = left_ref[...].astype(f32).T.astype(bf16)
        wt[two : 2 * two, :] = right_ref[...].astype(f32).T.astype(bf16)
        token_lane = lax.broadcasted_iota(jnp.int32, (1, tokens), 1)
        chunk = 256

        def step(t, carry):
            valid = valid_ref[...]
            valid_own = jnp.sum(jnp.where(token_lane == own + t, valid, 0.0), axis=1, keepdims=True)
            for start in range(0, tokens, chunk):
                x = pair_ref[t, start : start + chunk, :].astype(f32)
                normed = (norm_lanes(x) * gain).astype(bf16)
                mask = valid[:, start : start + chunk] * valid_own
                for side in range(2):
                    hidden = lax.dot_general(
                        wt[side * two : (side + 1) * two, :], normed, NT, preferred_element_type=f32
                    )
                    gated = jax.nn.sigmoid(hidden[:channels]) * hidden[channels:] * mask
                    send_a[t, side, :, start : start + chunk] = gated.astype(bf16)
            pl.when(t == 0)(lambda: pl.semaphore_wait(barrier, cols - 1 + rows - 1))
            ex_a.start(t)
            return carry

        lax.fori_loop(0, flat, step, 0)

    def pair_rows():
        row_f[tokens : tokens + 8, :] = jnp.zeros((8, channels), f32)

        def step(t, carry):
            row_f[0:tokens, :] = pair_ref[t].astype(f32)

            def piece(n, inner):
                a = n // cols
                c = lax.rem(n, cols)
                send_p[c, t, a] = row_f[pl.ds(n * flat, 8), :].astype(bf16)
                return inner

            lax.fori_loop(0, rows * cols, piece, 0, unroll=8)
            return carry

        lax.fori_loop(0, flat, step, 0)
        ex_p.start()

    def tokens_in():
        proj[...] = (
            jnp.dot(single_ref[...], token_ref[...], preferred_element_type=f32)
            .astype(bf16)
            .astype(f32)
        )
        lane = lax.broadcasted_iota(jnp.int32, (own_rows, 128), 1)

        def window(start, at):
            base = start // 128 * 128
            offset = start - base
            size = 128 if offset + head <= 128 else 256
            x = proj[:, base : base + size]
            shift = (at - offset) % size
            if shift:
                x = pltpu.roll(x, shift, 1)
            return x[:, :128]

        first = lane < head
        second = (lane >= head) & (lane < 2 * head)
        ones = jnp.where(lane == 2 * head, 1.0, 0.0)
        for h in range(heads):
            q = window(h * head, head)
            k = window(width + h * head, head)
            v = window(2 * width + h * head, 0)
            send_q[h, :, 0:128] = jnp.where(second, q, 0.0).astype(bf16)
            send_q[h, :, 128:256] = jnp.where(first, v, jnp.where(second, k, ones)).astype(bf16)
        ex_q.start()

    def to_channels():
        recv_l[:, block:128, :] = jnp.zeros((rows, 128 - block, tokens), bf16)

        def step(t, carry):
            ex_a.wait_recv(t)
            for side in range(2):
                send_b[:, side, span(t, cols), :] = swap01(recv_a[:, t, side])
            ex_l.start(t)
            ex_r.start(t)
            return carry

        lax.fori_loop(0, flat, step, 0)

    def to_samples():
        ex_q.wait_recv()

        def step(t, carry):
            x = swap01(recv_q[:, span(t, samples), :])
            query[:, span(t, cols), :] = x[:, :, 0:128]
            send_k[:, span(t, cols), :] = x[:, :, 128:256]
            return carry

        lax.fori_loop(0, flat, step, 0)
        ex_k.start()

    def pair_columns():
        ex_p.wait_recv()

        def step(n, carry):
            a = n // flat
            t = lax.rem(n, flat)
            pair_j[a, :, span(t, cols), :] = swap01(recv_p[:, t, a])
            return carry

        lax.fori_loop(0, rows * flat, step, 0)

    def gates():
        def step(n, carry):
            a = n // flat
            t = lax.rem(n, flat)
            normed = (norm_lanes(pair_j[a, t].astype(f32)) * gain).astype(bf16)
            gate_j[n] = jax.nn.sigmoid(jnp.dot(normed, gate_ref[...], preferred_element_type=f32))
            return carry

        lax.fori_loop(0, rows * flat, step, 0)

    def triangle():
        def ready(t, carry):
            ex_l.wait_recv(t)
            ex_r.wait_recv(t)
            return carry

        lax.fori_loop(0, flat, ready, 0)

        def step(n, carry):
            rhs = recv_r[pl.ds(n * group, group)].reshape(group * block, tokens)
            for r in range(0, rows, 2):
                lhs = recv_l[r : r + 2].reshape(256, tokens)
                mixed = lax.dot_general(rhs, lhs, NT, preferred_element_type=f32).astype(bf16)
                send_c[r, span(n, group * block), :] = mixed[:, 0:128]
                send_c[r + 1, span(n, group * block), :] = mixed[:, 128:256]
            ex_c.start(n)
            return carry

        lax.fori_loop(0, mixes, step, 0)

    def to_pairs():
        def step(n, carry):
            ex_c.wait_recv(n)

            def piece(k, inner):
                m = n * group * flat + k
                send_d[:, m] = swap01(recv_c[:, span(m, cols), :])
                return inner

            lax.fori_loop(0, group * flat, piece, 0)
            ex_d.start(n)
            return carry

        lax.fori_loop(0, mixes, step, 0)

    def update():
        mix_gain = mix_gain_ref[...].T
        bias_w = bias_ref[...]
        bias_j[...] = jnp.zeros(bias_j.shape, f32)

        def columns(a):
            new = []
            for t in range(flat):
                n = a * flat + t
                mixed = recv_d[n].astype(f32)
                centered = mixed - jnp.mean(mixed, axis=0, keepdims=True)
                variance = jnp.mean(centered * centered, axis=0, keepdims=True)
                mixed_norm = (centered * lax.rsqrt(variance + epsilon) * mix_gain).astype(bf16)
                change = lax.dot_general(mixed_norm, out_w_ref[...], TN, preferred_element_type=f32)
                pair_new = pair_j[a, t].astype(f32) + gate_j[n] * change[:block]
                pair_new = pair_new.astype(bf16).astype(f32)
                new.append(pair_new)
                bias_input = norm_lanes(pair_new).astype(bf16)
                bias_j[a, t, :, 0:block] = lax.dot_general(
                    bias_w, bias_input, NT, preferred_element_type=f32
                )
            zero = jnp.zeros((block, channels), f32)
            stacked = swap01(jnp.stack(new + [zero] * (8 - flat), axis=0))
            for t in range(flat):
                part = stacked[t * cols : (t + 1) * cols, 0:flat, :]
                tiles_out[:, t, a] = part.astype(bf16)
            send_e[:, a] = swap01(bias_j[a])

        def step(n, carry):
            ex_d.wait_recv(n)

            def one(k, inner):
                columns(n * group + k)
                return inner

            lax.fori_loop(0, group, one, 0)
            ex_e.start(n)
            return carry

        lax.fori_loop(0, mixes, step, 0)

    def biases():
        for n in range(mixes):
            ex_e.wait_recv(n)
        for a in range(rows):
            x = swap01(recv_e[:, a])
            bias_t[a * block : (a + 1) * block, :] = x[0:flat].reshape(block, 128)
        for n in range(tokens // 128):
            at = slice(n * 128, (n + 1) * 128)
            bias_s[:, at] = bias_t[at, :].T[0:block] + forbid_ref[:, at]

    def attend():
        score_scale = 1.0 / math.sqrt(head)

        def step(s, carry):
            keys = recv_k[:, s].reshape(tokens, 128)
            scores = lax.dot_general(query[s], keys, NT, preferred_element_type=f32)
            scores = scores * score_scale + bias_s[...]
            row_max = jnp.max(scores, axis=-1, keepdims=True)
            weights = jnp.exp(scores - row_max).astype(bf16)
            summed = jnp.dot(weights, keys, preferred_element_type=f32)
            att[s] = (summed / summed[:, 2 * head : 2 * head + 1]).astype(bf16)
            return carry

        lax.fori_loop(0, samples, step, 0)

    def to_tokens():
        def step(t, carry):
            send_f[:, span(t, samples), :] = swap01(att[:, span(t, cols), :])
            return carry

        lax.fori_loop(0, flat, step, 0)
        ex_f.start()

    def merge():
        merged = jnp.zeros((own_rows, width), f32)
        for h in range(heads):
            merged = merged + jnp.dot(
                recv_f[h][:, :head],
                merge_ref[h * head : (h + 1) * head, :],
                preferred_element_type=f32,
            )
        attn_out[...] = swap01(merged.reshape(flat, samples, width)).astype(bf16)

    greet("col", cols)
    greet("row", rows)
    project()
    tokens_in()
    pair_rows()
    to_channels()
    to_samples()
    pair_columns()
    gates()
    triangle()
    to_pairs()
    update()
    biases()
    ex_k.wait_recv()
    attend()
    to_tokens()
    ex_f.wait_recv()
    merge()
    for ex in (ex_a, ex_p, ex_q, ex_l, ex_r, ex_k, ex_c, ex_d, ex_e, ex_f):
        ex.wait_send()


def shards(
    pair_state,
    single_rep,
    token_mask,
    chain_ids,
    pair_gain,
    mix_gain,
    left_weight,
    right_weight,
    gate_weight,
    out_weight,
    bias_weight,
    token_weight,
    merge_weight,
):
    rows = lax.axis_size("row")
    cols = lax.axis_size("col")
    row_index = lax.axis_index("row")
    flat, tokens, channels = pair_state.shape
    samples, _, width = single_rep.shape
    heads = bias_weight.shape[1]
    block = flat * cols

    def key_order(x):
        return x.reshape(rows, cols, flat).transpose(0, 2, 1)

    ids = key_order(jnp.arange(tokens, dtype=jnp.int32))
    chains = key_order(chain_ids)
    valid = token_mask == 1
    ids_rows = lax.dynamic_index_in_dim(ids, row_index, 0, False).reshape(block)
    chain_rows = lax.dynamic_index_in_dim(chains, row_index, 0, False).reshape(block)
    allowed = key_order(valid).reshape(1, tokens) & (
        chain_rows[:, None] == chains.reshape(1, tokens)
    ) | (ids_rows[:, None] == ids.reshape(1, tokens))
    forbid = jnp.where(allowed, 0.0, -1e30).astype(f32)
    single_rows = single_rep.transpose(1, 0, 2).reshape(flat * samples, width)

    def vmem(*shape, dtype=bf16):
        return pltpu.VMEM(shape, dtype)

    own_rows = flat * samples
    ch8 = channels // cols
    pieces = rows * flat
    scratch = [
        vmem(4 * channels, channels),
        vmem(flat, 2, channels, tokens),
        vmem(cols, flat, 2, ch8, tokens),
        vmem(ch8, 2, block, tokens),
        vmem(rows, 128, tokens),
        vmem(rows, block, tokens),
        vmem(rows, tokens, 128),
        vmem(rows, tokens, 128),
        vmem(cols, pieces, ch8, 128),
        vmem(pieces, channels, 128),
        vmem(tokens + 8, channels, dtype=f32),
        vmem(cols, flat, rows, 8, channels),
        vmem(cols, flat, rows, 8, channels),
        vmem(rows, 8, block, channels),
        vmem(pieces, block, channels, dtype=f32),
        vmem(own_rows, 3 * width, dtype=f32),
        vmem(cols, own_rows, 256),
        vmem(cols, own_rows, 256),
        vmem(samples, block, 128),
        vmem(samples, block, 128),
        vmem(rows, samples, block, 128),
        vmem(rows, 8, heads, 128, dtype=f32),
        vmem(cols, rows, 8, 128, dtype=f32),
        vmem(cols, rows, 8, 128, dtype=f32),
        vmem(tokens, 128, dtype=f32),
        vmem(block, tokens, dtype=f32),
        vmem(samples, block, 128),
        vmem(cols, own_rows, 128),
        vmem(cols, own_rows, 128),
    ]
    mixes = pair_groups(rows)
    for size, chunks in (
        (cols, flat),
        (cols, 1),
        (cols, 1),
        (rows, flat),
        (rows, flat),
        (rows, 1),
        (rows, mixes),
        (cols, mixes),
        (cols, mixes),
        (cols, 1),
    ):
        scratch += [
            pltpu.SemaphoreType.DMA((chunks, size)),
            pltpu.SemaphoreType.DMA((chunks, size)),
            pltpu.SemaphoreType.DMA((chunks,)),
        ]
    whole = pl.BlockSpec(memory_space=pltpu.VMEM)
    tiles, attention_out = pl.pallas_call(
        functools.partial(kernel, rows, cols),
        out_shape=(
            jax.ShapeDtypeStruct((cols, flat, rows, flat, channels), bf16),
            jax.ShapeDtypeStruct((samples, flat, width), bf16),
        ),
        in_specs=[whole] * 13,
        out_specs=(whole, whole),
        scratch_shapes=scratch,
        compiler_params=pltpu.CompilerParams(
            collective_id=0, has_side_effects=True, vmem_limit_bytes=60 * 1024 * 1024
        ),
    )(
        pair_state,
        single_rows,
        valid.astype(f32).reshape(1, tokens),
        forbid,
        pair_gain.reshape(1, channels),
        mix_gain.reshape(1, channels),
        left_weight,
        right_weight,
        gate_weight,
        out_weight,
        bias_weight.T,
        token_weight,
        merge_weight,
    )
    return tiles.reshape(block, rows, 1, flat, channels), attention_out


def solution(mesh):
    in_specs = (
        P(("row", "col"), None, None),
        P(None, ("row", "col"), None),
        P(),
        P(),
        P(),
        P(),
        P(),
        P(),
        P(),
        P(),
        P(),
        P(),
        P(),
    )
    out_specs = (P("row", None, "col", None, None), P(None, ("row", "col"), None))
    return jax.shard_map(shards, mesh=mesh, in_specs=in_specs, out_specs=out_specs, check_vma=False)
```
